256 devices in a mesh: rows: 256 (over y, z, x, core).
Axes of the slice: x: 4, y: 4, z: 8, core: 2. Of those that a mesh axis runs over, the one named last changes fastest.
Arguments:
- embeddings: bfloat16 [524288, 128], P('rows'), may hold values from -24 to 24
- labels: int32 [524288], P('rows'), may hold values from 0 to 64
- predictions: float32 [64, 524288], P(None, 'rows'), may hold values from -25 to 25
- coefficients: float32 [64, 524288], P(None, 'rows'), may hold values from -4 to 4
- block_index: int32 [2, 1024], replicated, may hold values from 0 to 2047, as said below
- owner_id: int32 [2], replicated, may hold values from 0 to 255
Outputs:
- new_predictions: float32 [64, 524288], P(None, 'rows')
- new_coefficients: float32 [64, 524288], P(None, 'rows')
- residual_norms: float32 [2, 64], replicated
The draws below stay inside these ranges and needn't reach their ends.
Inputs may be any that keep to these rules, and one draw needn't show every extreme that they name: `block_index`: within each step the 1024 entries are distinct local rows of the owner; 0 and 2047 appear in every step.
All inputs are finite; a program needn't handle non-finite values.
Results may differ from the reference program's by a relative error of at most 0.008.
Values may be sent and summed in bfloat16 or wider, within the bound.
A program may use at most 128 MiB of HBM per device.

```python
import jax
import jax.numpy as jnp
from jax import lax

FEATURES = 128
TARGETS = 64
BLOCK = 1024
STEPS = 2
ROWS_DEV = 2048
TOTAL_ROWS = 524288
CLASSES = 65
N_ROWS = 256


def draw_embeddings(key, part):
    pick_key, scale_key, value_key = jax.random.split(key, 3)
    order = jax.random.permutation(pick_key, FEATURES)
    strong = order < FEATURES // 8
    strong_scale = jax.random.uniform(scale_key, (FEATURES,), jnp.float32, 3.0, 4.0)
    scales = jnp.where(strong, strong_scale, 0.45)
    values = jnp.clip(jax.random.normal(value_key, (TOTAL_ROWS, FEATURES), jnp.float32), -6.0, 6.0)
    return (values * scales[None, :]).astype(jnp.bfloat16)


def draw_predictions(key, part):
    noise_key = jax.random.fold_in(key, 0)
    position = jnp.arange(TOTAL_ROWS, dtype=jnp.float32)[None, :] / TOTAL_ROWS
    jitter = jax.random.normal(noise_key, (TARGETS, TOTAL_ROWS), jnp.float32)
    return jnp.clip(jitter, -5.0, 5.0) * (1.0 + 2.0 * position)


def draw_block_index(key, part):
    step_keys = jax.random.split(key, STEPS)

    def one_draw(subkey):
        order_key, mix_key = jax.random.split(subkey)
        interior = jax.random.permutation(order_key, ROWS_DEV - 2)[:BLOCK - 2].astype(jnp.int32) + 1
        entire = jnp.concatenate([jnp.array([0, ROWS_DEV - 1], jnp.int32), interior])
        return jax.random.permutation(mix_key, entire).astype(jnp.int32)
    return jax.vmap(one_draw)(step_keys)


def place_ends(values, stream_key, low, high):
    longest = values.shape.index(max(values.shape))
    spots = []
    for shift in (0, 1):
        where = [jax.random.randint(jax.random.fold_in(stream_key, axis), (), 0, length) for axis, length in enumerate(values.shape)]
        where[longest] = (where[longest] + shift) % values.shape[longest]
        spots.append(tuple(where))
    return values.at[spots[0]].set(low).at[spots[1]].set(high)


def block_scale(own_key, shape, shards, least, top_value):
    level = 1.0
    for dim, parts in shards:
        heights = jax.random.uniform(jax.random.fold_in(jax.random.fold_in(own_key, 6), dim), (parts,), jnp.float32, least / len(shards), top_value / len(shards))
        level = level * jnp.repeat(jnp.exp(heights), shape[dim] // parts).reshape((-1,) + (1,) * (len(shape) - 1 - dim))
    return level


def centred(key, shape, spread, limit, cuts=(), kind=jnp.bfloat16):
    loudness = block_scale(key, shape, cuts, -0.22, 0.18) if cuts else 1.0
    values = jax.random.normal(key, shape, jnp.float32) * spread * loudness
    return jnp.minimum(jnp.maximum(values, -limit), limit).astype(kind)


def setup_inputs(seed: int = 0) -> dict:
    arg_keys = jax.random.split(jax.random.key(seed), 7)
    embeddings = draw_embeddings(jax.random.fold_in(arg_keys[6], 71), 0)
    labels = place_ends(jax.random.randint(arg_keys[1], (TOTAL_ROWS,), 0, CLASSES), jax.random.fold_in(arg_keys[1], 1), 0, CLASSES - 1).astype(jnp.int32)
    predictions = draw_predictions(jax.random.fold_in(arg_keys[6], 71), 0)
    coefficients = centred(arg_keys[3], (TARGETS, TOTAL_ROWS), 0.5, 4.0, ((1, 256),), jnp.float32)
    block_index = draw_block_index(jax.random.fold_in(arg_keys[6], 71), 0)
    owner_id = jax.random.randint(arg_keys[5], (STEPS,), 0, N_ROWS).astype(jnp.int32)
    return {"embeddings": embeddings, "labels": labels, "predictions": predictions, "coefficients": coefficients, "block_index": block_index, "owner_id": owner_id}


RIDGE = 1.0

def squares_of(points):
    widened = points.astype(jnp.float32)
    return lax.optimization_barrier(jnp.sum(widened * widened, axis=1))

def kernel_tile(left_points, left_norms, right_points, right_norms):
    cross_term = lax.dot_general(left_points.astype(jnp.float32), right_points.astype(jnp.float32), (((1,), (1,)), ((), ())), preferred_element_type=jnp.float32)
    distance = left_norms[:, None] + right_norms[None, :] - 2.0 * cross_term
    return jnp.exp(distance * (-0.5 / left_points.shape[1]))

def solve_block(gram_matrix, right_side):
    factor = jnp.linalg.cholesky(gram_matrix)
    middle = lax.linalg.triangular_solve(factor, right_side, left_side=False, lower=True, transpose_a=True)
    return lax.linalg.triangular_solve(factor, middle, left_side=False, lower=True, transpose_a=False)

def reference(embeddings, labels, predictions, coefficients, block_index, owner_id):
    thresholds = jnp.arange(TARGETS, dtype=jnp.int32)
    targets = (labels[None, :] <= thresholds[:, None]).astype(jnp.float32)
    row_norms = squares_of(embeddings)
    slab_points = embeddings.reshape(TOTAL_ROWS // ROWS_DEV, ROWS_DEV, FEATURES)
    slab_norms = row_norms.reshape(TOTAL_ROWS // ROWS_DEV, ROWS_DEV)
    eye_block = jnp.eye(BLOCK, dtype=jnp.float32)
    residual = targets - predictions - RIDGE * coefficients
    norm_list = []
    for iteration in range(STEPS):
        global_rows = (owner_id[iteration] * ROWS_DEV + block_index[iteration]).astype(jnp.int32)
        block_points = jnp.take(embeddings, global_rows, axis=0)
        block_norms = jnp.take(row_norms, global_rows, axis=0)
        block_residual = jnp.take(residual, global_rows, axis=1)
        gram_matrix = kernel_tile(block_points, block_norms, block_points, block_norms) + RIDGE * eye_block
        update_block = solve_block(gram_matrix, block_residual)
        coefficients = coefficients.at[:, global_rows].add(update_block)
        update_half = update_block.astype(jnp.bfloat16)

        def add_slab(pieces):
            kernel_block = kernel_tile(block_points, block_norms, pieces[0], pieces[1]).astype(jnp.bfloat16)
            return jnp.dot(update_half.astype(jnp.float32), kernel_block.astype(jnp.float32), preferred_element_type=jnp.float32)
        increment = lax.map(add_slab, (slab_points, slab_norms))
        predictions = predictions + jnp.transpose(increment, (1, 0, 2)).reshape(TARGETS, TOTAL_ROWS)
        residual = targets - predictions - RIDGE * coefficients
        norm_list.append(jnp.sqrt(lax.optimization_barrier(jnp.sum(residual * residual, axis=1)) / TOTAL_ROWS + 1e-06))
    return (predictions, coefficients, jnp.stack(norm_list))
```

```python
import functools

import jax
import jax.numpy as jnp
from jax import lax
from jax.experimental import pallas as pl
from jax.experimental.pallas import tpu as pltpu
from jax.sharding import PartitionSpec as P

F32, BF16, I32 = jnp.float32, jnp.bfloat16, jnp.int32
MESH = pl.DeviceIdType.MESH
NN = (((1,), (0,)), ((), ()))
NT = (((1,), (1,)), ((), ()))
TN = (((0,), (0,)), ((), ()))

RIDGE = 1.0
FEATURES = 128
TARGETS = 64
BLOCK = 1024
ROWS = 2048
NX, NY, NZ = 4, 4, 8
STRIDE_X, STRIDE_Z, STRIDE_Y = 2, 2 * NX, 2 * NX * NZ
PAY = 2048
NB = 256
STAGES = 7
VMEM_LIMIT = 60 << 20


def mm(a, b, dims=NN):
    return lax.dot_general(a, b, dims, preferred_element_type=F32)


def split(a):
    high = a.astype(BF16)
    return high, (a - high.astype(F32)).astype(BF16)


def mm3(a, b, dims=NN):
    return mm(a[0], b[0], dims) + (mm(a[0], b[1], dims) + mm(a[1], b[0], dims))


def iota(shape, dim):
    return lax.broadcasted_iota(I32, shape, dim)


def vmem():
    return pl.BlockSpec(memory_space=pltpu.VMEM)


def smem():
    return pl.BlockSpec(memory_space=pltpu.SMEM)


def residual_of(labels, predictions, coefficients):
    targets = (labels <= iota((TARGETS, labels.shape[1]), 0)).astype(F32)
    return targets - predictions - RIDGE * coefficients


def square_norms(points):
    wide = points.astype(F32)
    squares = wide * wide
    high, low = split(squares)
    ones = jnp.ones((8, points.shape[1]), BF16)
    row = (mm(ones, high, NT) + mm(ones, low, NT))[:1]
    return row, jnp.sum(squares, axis=1, keepdims=True)


def kernel_of(cross, left, right):
    return jnp.exp((left + right - 2.0 * cross) * (-0.5 / FEATURES))


def selection(picked, start, size):
    return (iota((size, picked.shape[1]), 0) + start == picked).astype(BF16)


def prep_kernel(owner_ref, points_ref, labels_ref, pred_ref, coef_ref, index_ref, out_ref):
    me = lax.axis_index("rows")
    for step in range(2):

        @pl.when(owner_ref[step] == me)
        def _():
            residual = residual_of(labels_ref[...], pred_ref[...], coef_ref[...])
            high, low = split(residual)
            picked = index_ref[step : step + 1, :]
            acc = jnp.zeros((256, BLOCK), F32)
            for start in range(0, ROWS, 256):
                rows = slice(start, start + 256)
                left = jnp.concatenate(
                    [points_ref[rows, :].T, high[:, rows], low[:, rows]], axis=0
                )
                acc = acc + mm(left, selection(picked, start, 256))
            for b in range(8):
                out_ref[step, b * 256 : (b + 1) * 256, :] = acc[:, b * 128 : (b + 1) * 128].astype(BF16)


def coords():
    me = lax.axis_index("rows")
    core = lax.rem(me, 2)
    x = lax.rem(lax.div(me, STRIDE_X), NX)
    z = lax.rem(lax.div(me, STRIDE_Z), NZ)
    y = lax.div(me, STRIDE_Y)
    return me, core, x, y, z


def peers(me, at, size, stride):
    out = []
    for hop in [d for k in range(1, size // 2 + 1) for d in ((k, -k) if 2 * k < size else (k,))]:
        position = lax.rem(at + hop + size, size)
        out.append((position, me + (position - at) * stride))
    return out


def spread_kernel(owner_ref, own_ref, out_ref, cand_c, cand_x, cand_y, cand_z, mine, send_sem, recv_sem):
    me, core, x, y, z = coords()
    other = me + 1 - 2 * core
    rings = ((peers(me, x, NX, STRIDE_X), x), (peers(me, y, NY, STRIDE_Y), y), (peers(me, z, NZ, STRIDE_Z), z))
    barrier = pltpu.get_barrier_semaphore()
    count = 1
    pl.semaphore_signal(barrier, inc=1, device_id=(other,), device_id_type=MESH)
    for ring, _ in rings:
        for _, device in ring:
            pl.semaphore_signal(barrier, inc=1, device_id=(device,), device_id_type=MESH)
            count += 1
    pl.semaphore_wait(barrier, count)

    owner = owner_ref[core]
    owner_at = (
        lax.rem(lax.div(owner, STRIDE_X), NX),
        lax.div(owner, STRIDE_Y),
        lax.rem(lax.div(owner, STRIDE_Z), NZ),
    )

    copy = pltpu.make_async_remote_copy(
        own_ref.at[1 - core], cand_c.at[core], send_sem.at[0, 0], recv_sem.at[0, 0],
        device_id=(other,), device_id_type=MESH,
    )
    copy.start()
    cand_c[core] = own_ref[core]
    copy.wait()

    held = cand_c
    held_at = lax.rem(owner, 2)
    size = PAY
    stages = (cand_x, cand_y, cand_z)
    for phase, (cand, (ring, at)) in enumerate(zip(stages, rings), 1):
        members = cand.shape[0]
        mine[0:size, :] = held[held_at]
        piece = size // members
        copies = []
        for position, device in ring:
            copy = pltpu.make_async_remote_copy(
                mine.at[pl.ds(pl.multiple_of(position * piece, piece), piece), :],
                cand.at[at], send_sem.at[phase, position], recv_sem.at[phase, at],
                device_id=(device,), device_id_type=MESH,
            )
            copy.start()
            copies.append(copy)
        cand[at] = mine[pl.ds(pl.multiple_of(at * piece, piece), piece), :]
        for copy in copies:
            copy.wait_send()
        for position, device in ring:
            pltpu.make_async_remote_copy(
                cand.at[position], cand.at[position], send_sem.at[phase, position],
                recv_sem.at[phase, position], device_id=(device,), device_id_type=MESH,
            ).wait_recv()
        held, held_at, size = cand, owner_at[phase - 1], piece

    start = x * (PAY // NX) + y * (PAY // NX // NY) + z * size
    out_ref[pl.ds(pl.multiple_of(start, size), size), :] = held[held_at]
    for phase, (ring, at), members in ((4, rings[2], NZ), (5, rings[1], NY), (6, rings[0], NX)):
        here = pl.ds(pl.multiple_of(start, size), size)
        base = start - at * size
        copies = []
        for position, device in ring:
            copy = pltpu.make_async_remote_copy(
                out_ref.at[here, :], out_ref.at[here, :], send_sem.at[phase, position],
                recv_sem.at[phase, at], device_id=(device,), device_id_type=MESH,
            )
            copy.start()
            copies.append(copy)
        for copy in copies:
            copy.wait_send()
        for position, device in ring:
            there = pl.ds(pl.multiple_of(base + position * size, size), size)
            pltpu.make_async_remote_copy(
                out_ref.at[there, :], out_ref.at[there, :], send_sem.at[phase, position],
                recv_sem.at[phase, position], device_id=(device,), device_id_type=MESH,
            ).wait_recv()
        start, size = base, size * members


def unpack_points(pay_ref):
    return jnp.concatenate([pay_ref[b * 256 : b * 256 + 128, :].T for b in range(8)], axis=0)


def unpack_residual(pay_ref, part):
    lo = 128 + 64 * part
    return jnp.concatenate([pay_ref[b * 256 + lo : b * 256 + lo + 64, :] for b in range(8)], axis=1)


def inverse(matrix):
    n = matrix.shape[0]
    eye = (iota((n, n), 0) == iota((n, n), 1)).astype(F32)
    top = jnp.max(jnp.sum(jnp.abs(matrix), axis=0, keepdims=True), axis=1, keepdims=True)
    gain = 2.0 / (1.0 + top)
    rest = eye - gain * matrix
    scale = (top + 1.0) / jnp.maximum(top - 1.0, 1e-2)
    c = 1.0 + 1.0 / (2.0 * scale * scale - 1.0)
    result = (c * gain) * (eye + rest)
    parts = split(rest)
    for _ in range(STAGES - 1):
        rest = c * mm3(parts, parts) - (c - 1.0) * eye
        scale = jnp.minimum(2.0 * scale * scale - 1.0, 1e4)
        c = 1.0 + 1.0 / (2.0 * scale * scale - 1.0)
        parts = split(rest)
        result = c * (result + mm3(split(result), parts))
    return result


def block(k):
    return slice(k * NB, (k + 1) * NB)


def forward(k, v_ref, u_ref, xh_ref, xl_ref, wh_ref, wl_ref):
    v = split(v_ref[:, block(k)])
    if (k + 1) * NB < BLOCK:
        rest = slice((k + 1) * NB, BLOCK)
        v_ref[:, rest] = v_ref[:, rest] - mm3(v, (wh_ref[block(k), rest], wl_ref[block(k), rest]))
    u_ref[:, block(k)] = mm3(v, (xh_ref[k], xl_ref[k]))


def backward(u_ref, wh_ref, wl_ref):
    for j in range(BLOCK // NB - 1, 0, -1):
        u = split(u_ref[:, block(j)])
        for k in range(j):
            w = (wh_ref[block(k), block(j)], wl_ref[block(k), block(j)])
            u_ref[:, block(k)] = u_ref[:, block(k)] - mm3(u, w, NT)


def solve_kernel(pay_ref, points_ref, u_ref, xh_ref, xl_ref, wh_ref, wl_ref, g_ref, v_ref, uf_ref):
    points_ref[...] = unpack_points(pay_ref)
    norm_row, norm_col = square_norms(points_ref[...])
    count = BLOCK // NB
    for i in range(count):
        cross = mm(points_ref[block(i), :], points_ref[i * NB :, :], NT)
        tile = kernel_of(cross, norm_col[block(i)], norm_row[:, i * NB :])
        diagonal = (iota(tile.shape, 0) == iota(tile.shape, 1)).astype(F32)
        g_ref[block(i), i * NB :] = tile + RIDGE * diagonal
    v_ref[...] = unpack_residual(pay_ref, 0).astype(F32) + unpack_residual(pay_ref, 1).astype(F32)
    for k in range(count):
        x = split(inverse(g_ref[block(k), block(k)]))
        xh_ref[k], xl_ref[k] = x
        if k + 1 < count:
            rest = slice((k + 1) * NB, BLOCK)
            g = split(g_ref[block(k), rest])
            w = split(mm3(x, g))
            wh_ref[block(k), rest], wl_ref[block(k), rest] = w
            for i in range(k + 1, count):
                lo = (i - k - 1) * NB
                gi = (g[0][:, lo : lo + NB], g[1][:, lo : lo + NB])
                wi = (w[0][:, lo:], w[1][:, lo:])
                g_ref[block(i), i * NB :] = g_ref[block(i), i * NB :] - mm3(gi, wi, TN)
        forward(k, v_ref, uf_ref, xh_ref, xl_ref, wh_ref, wl_ref)
    backward(uf_ref, wh_ref, wl_ref)
    high, low = split(uf_ref[...])
    u_ref[0:TARGETS, :] = high
    u_ref[TARGETS:, :] = low


def swap_kernel(*refs):
    count = (len(refs) - 2) // 2
    sources, targets = refs[:count], refs[count : 2 * count]
    send_sem, recv_sem = refs[2 * count :]
    me = lax.axis_index("rows")
    other = me + 1 - 2 * lax.rem(me, 2)
    barrier = pltpu.get_barrier_semaphore()
    pl.semaphore_signal(barrier, inc=1, device_id=(other,), device_id_type=MESH)
    pl.semaphore_wait(barrier, 1)
    copies = []
    for i in range(count):
        copy = pltpu.make_async_remote_copy(
            sources[i], targets[i], send_sem.at[i], recv_sem.at[i],
            device_id=(other,), device_id_type=MESH,
        )
        copy.start()
        copies.append(copy)
    for copy in copies:
        copy.wait()


def swap(arrays, collective_id):
    return pl.pallas_call(
        swap_kernel,
        out_shape=[jax.ShapeDtypeStruct(a.shape, a.dtype) for a in arrays],
        in_specs=[vmem()] * len(arrays),
        out_specs=[vmem()] * len(arrays),
        scratch_shapes=[pltpu.SemaphoreType.DMA((len(arrays),)), pltpu.SemaphoreType.DMA((len(arrays),))],
        compiler_params=pltpu.CompilerParams(collective_id=collective_id, has_side_effects=True),
        name="swap",
    )(*arrays)


def second_kernel(
    owner_ref, pay_ref, mine_ref, first_ref, u1_ref, index_ref, xh_ref, xl_ref, wh_ref, wl_ref,
    u_ref, v_ref, uf_ref,
):
    core = lax.rem(lax.axis_index("rows"), 2)

    @pl.when(core == 1)
    def _():
        right, _ = square_norms(mine_ref[...])
        _, left = square_norms(first_ref[...])
        v = unpack_residual(pay_ref, 0).astype(F32) + unpack_residual(pay_ref, 1).astype(F32)
        for i in range(0, BLOCK, 256):
            rows = slice(i, i + 256)
            cross = mm(first_ref[rows, :], mine_ref[...], NT)
            half = kernel_of(cross, left[rows], right).astype(BF16)
            v = v - mm(u1_ref[0:TARGETS, rows], half)
        v_ref[...] = v

    @pl.when((core == 1) & (owner_ref[0] == owner_ref[1]))
    def _():
        placed = place(u1_ref[...], index_ref[0:1, :]).astype(BF16)
        both = jnp.zeros((2 * TARGETS, BLOCK), F32)
        for start in range(0, ROWS, 256):
            both = both + mm(placed[:, start : start + 256], selection(index_ref[1:2, :], start, 256))
        v_ref[...] = v_ref[...] - RIDGE * (both[:TARGETS] + both[TARGETS:])

    @pl.when(core == 1)
    def _():
        for k in range(BLOCK // NB):
            forward(k, v_ref, uf_ref, xh_ref, xl_ref, wh_ref, wl_ref)
        backward(uf_ref, wh_ref, wl_ref)
        high, low = split(uf_ref[...])
        u_ref[0:TARGETS, :] = high
        u_ref[TARGETS:, :] = low


def place(update, picked):
    return jnp.concatenate(
        [mm(update, selection(picked, start, 256), NT) for start in range(0, ROWS, 256)], axis=1
    )


def apply_kernel(
    owner_ref, rows_ref, labels_ref, pred_ref, coef_ref, index_ref, pm_ref, po_ref, um_ref, uo_ref, vo_ref,
    new_pred_ref, new_coef_ref, sums_ref, block_ref, half_ref,
):
    me = lax.axis_index("rows")
    core = lax.rem(me, 2)

    @pl.when(core == 0)
    def _():
        block_ref[0] = pm_ref[...]
        block_ref[1] = po_ref[...]
        half_ref[0] = um_ref[...]
        half_ref[1] = vo_ref[...]

    @pl.when(core == 1)
    def _():
        block_ref[0] = po_ref[...]
        block_ref[1] = pm_ref[...]
        half_ref[0] = uo_ref[...]
        half_ref[1] = um_ref[...]

    right, _ = square_norms(rows_ref[...])
    new_coef_ref[...] = coef_ref[...]
    columns = []
    for step in range(2):

        @pl.when(owner_ref[step] == me)
        def _():
            both = place(half_ref[step], index_ref[step : step + 1, :])
            new_coef_ref[...] = new_coef_ref[...] + (both[:TARGETS] + both[TARGETS:])

        _, left = square_norms(block_ref[step])
        before = pred_ref if step == 0 else new_pred_ref
        total = jnp.zeros((TARGETS, 1), F32)
        for start in range(0, ROWS, 256):
            cols = slice(start, start + 256)
            cross = mm(block_ref[step], rows_ref[cols, :], NT)
            half = kernel_of(cross, left, right[:, cols]).astype(BF16)
            new = before[:, cols] + mm(half_ref[step, 0:TARGETS, :], half)
            new_pred_ref[:, cols] = new
            residual = residual_of(labels_ref[:, cols], new, new_coef_ref[:, cols])
            total = total + jnp.sum(residual * residual, axis=1, keepdims=True)
        columns.append(total)
    sums = jnp.broadcast_to(jnp.concatenate(columns, axis=0), (128, 128))
    sums_ref[...] = sums.T[0:8, :]


def norm_kernel(total_rows, sums_ref, out_ref, got_a, got_y, got_z, send_sem, recv_sem):
    me, core, x, y, z = coords()
    here = core + 2 * x
    plane = []
    for hop in range(1, 2 * NX):
        position = lax.rem(here + hop, 2 * NX)
        plane.append((position, me + position - here))
    rings = (
        (plane, here, got_a),
        (peers(me, y, NY, STRIDE_Y), y, got_y),
        (peers(me, z, NZ, STRIDE_Z), z, got_z),
    )
    barrier = pltpu.get_barrier_semaphore()
    count = 0
    for ring, _, _ in rings:
        for _, device in ring:
            pl.semaphore_signal(barrier, inc=1, device_id=(device,), device_id_type=MESH)
            count += 1
    pl.semaphore_wait(barrier, count)
    value = sums_ref[...]
    for phase, (ring, at, got) in enumerate(rings):
        got[at] = value
        copies = []
        for position, device in ring:
            copy = pltpu.make_async_remote_copy(
                got.at[at], got.at[at], send_sem.at[phase, position], recv_sem.at[phase, at],
                device_id=(device,), device_id_type=MESH,
            )
            copy.start()
            copies.append(copy)
        for copy in copies:
            copy.wait_send()
        for position, device in ring:
            pltpu.make_async_remote_copy(
                got.at[position], got.at[position], send_sem.at[phase, position],
                recv_sem.at[phase, position], device_id=(device,), device_id_type=MESH,
            ).wait_recv()
        value = jnp.sum(got[...], axis=0)
    norms = jnp.sqrt(value / total_rows + 1e-06)
    out_ref[0:1, :] = norms[0:1, 0:TARGETS]
    out_ref[1:2, :] = norms[0:1, TARGETS:]


def local(embeddings, labels, predictions, coefficients, block_index, owner_id):
    shape = jax.ShapeDtypeStruct
    total_rows = embeddings.shape[0] * lax.axis_size("rows")
    labels = labels.reshape(1, ROWS)
    params = pltpu.CompilerParams(vmem_limit_bytes=VMEM_LIMIT)

    own = pl.pallas_call(
        prep_kernel,
        out_shape=shape((2, PAY, 128), BF16),
        in_specs=[smem()] + [vmem()] * 5,
        out_specs=vmem(),
        compiler_params=params,
        name="prep",
    )(owner_id, embeddings, labels, predictions, coefficients, block_index)

    pay = pl.pallas_call(
        spread_kernel,
        out_shape=shape((PAY, 128), BF16),
        in_specs=[smem(), vmem()],
        out_specs=vmem(),
        scratch_shapes=[
            pltpu.VMEM((2, PAY, 128), BF16),
            pltpu.VMEM((NX, PAY // NX, 128), BF16),
            pltpu.VMEM((NY, PAY // NX // NY, 128), BF16),
            pltpu.VMEM((NZ, PAY // NX // NY // NZ, 128), BF16),
            pltpu.VMEM((PAY, 128), BF16),
            pltpu.SemaphoreType.DMA((7, 8)),
            pltpu.SemaphoreType.DMA((7, 8)),
        ],
        compiler_params=pltpu.CompilerParams(
            collective_id=0, has_side_effects=True, vmem_limit_bytes=VMEM_LIMIT
        ),
        name="spread",
    )(owner_id, own)

    count = BLOCK // NB
    points, update, xh, xl, wh, wl = pl.pallas_call(
        solve_kernel,
        out_shape=[
            shape((BLOCK, FEATURES), BF16),
            shape((2 * TARGETS, BLOCK), BF16),
            shape((count, NB, NB), BF16),
            shape((count, NB, NB), BF16),
            shape((BLOCK, BLOCK), BF16),
            shape((BLOCK, BLOCK), BF16),
        ],
        in_specs=[vmem()],
        out_specs=[vmem()] * 6,
        scratch_shapes=[
            pltpu.VMEM((BLOCK, BLOCK), F32),
            pltpu.VMEM((TARGETS, BLOCK), F32),
            pltpu.VMEM((TARGETS, BLOCK), F32),
        ],
        compiler_params=params,
        name="solve",
    )(pay)

    other_points, other_update = swap([points, update], 1)

    second = pl.pallas_call(
        second_kernel,
        out_shape=shape((2 * TARGETS, BLOCK), BF16),
        in_specs=[smem()] + [vmem()] * 9,
        out_specs=vmem(),
        scratch_shapes=[pltpu.VMEM((TARGETS, BLOCK), F32), pltpu.VMEM((TARGETS, BLOCK), F32)],
        compiler_params=params,
        name="second",
    )(owner_id, pay, points, other_points, other_update, block_index, xh, xl, wh, wl)

    (other_second,) = swap([second], 2)
    core = lax.rem(lax.axis_index("rows"), 2)
    mine = jnp.where(core == 0, update, second)

    new_pred, new_coef, sums = pl.pallas_call(
        apply_kernel,
        out_shape=[
            shape((TARGETS, ROWS), F32),
            shape((TARGETS, ROWS), F32),
            shape((8, 128), F32),
        ],
        in_specs=[smem()] + [vmem()] * 10,
        out_specs=[vmem()] * 3,
        scratch_shapes=[
            pltpu.VMEM((2, BLOCK, FEATURES), BF16),
            pltpu.VMEM((2, 2 * TARGETS, BLOCK), BF16),
        ],
        compiler_params=params,
        name="apply",
    )(
        owner_id, embeddings, labels, predictions, coefficients, block_index,
        points, other_points, mine, other_update, other_second,
    )

    norms = pl.pallas_call(
        functools.partial(norm_kernel, total_rows),
        out_shape=shape((2, TARGETS), F32),
        in_specs=[vmem()],
        out_specs=vmem(),
        scratch_shapes=[
            pltpu.VMEM((2 * NX, 8, 128), F32),
            pltpu.VMEM((NY, 8, 128), F32),
            pltpu.VMEM((NZ, 8, 128), F32),
            pltpu.SemaphoreType.DMA((3, 8)),
            pltpu.SemaphoreType.DMA((3, 8)),
        ],
        compiler_params=pltpu.CompilerParams(collective_id=3, has_side_effects=True),
        name="norms",
    )(sums)
    return new_pred, new_coef, norms


def solution(mesh):
    in_specs = (P("rows", None), P("rows"), P(None, "rows"), P(None, "rows"), P(), P())
    out_specs = (P(None, "rows"), P(None, "rows"), P())
    return jax.shard_map(local, mesh=mesh, in_specs=in_specs, out_specs=out_specs, check_vma=False)
```

```python
import functools

import jax
import jax.numpy as jnp
from jax import lax
from jax.experimental import pallas as pl
from jax.experimental.pallas import tpu as pltpu
from jax.sharding import PartitionSpec as P

F32, BF16, I32 = jnp.float32, jnp.bfloat16, jnp.int32
MESH = pl.DeviceIdType.MESH
NN = (((1,), (0,)), ((), ()))
NT = (((1,), (1,)), ((), ()))
TN = (((0,), (0,)), ((), ()))

RIDGE = 1.0
FEATURES = 128
TARGETS = 64
BLOCK = 1024
ROWS = 2048
NX, NY, NZ = 4, 4, 8
STRIDE_X, STRIDE_Z, STRIDE_Y = 2, 2 * NX, 2 * NX * NZ
NB = 256
STAGES = 7
VMEM_LIMIT = 60 << 20


def mm(a, b, dims=NN):
    return lax.dot_general(a, b, dims, preferred_element_type=F32)


def split(a):
    high = a.astype(BF16)
    return high, (a - high.astype(F32)).astype(BF16)


def mm3(a, b, dims=NN):
    return mm(a[0], b[0], dims) + (mm(a[0], b[1], dims) + mm(a[1], b[0], dims))


def iota(shape, dim):
    return lax.broadcasted_iota(I32, shape, dim)


def vmem():
    return pl.BlockSpec(memory_space=pltpu.VMEM)


def smem():
    return pl.BlockSpec(memory_space=pltpu.SMEM)


def residual_of(labels, predictions, coefficients):
    targets = (labels <= iota((TARGETS, labels.shape[1]), 0)).astype(F32)
    return targets - predictions - RIDGE * coefficients


def square_norms(points):
    wide = points.astype(F32)
    squares = wide * wide
    high, low = split(squares)
    ones = jnp.ones((8, points.shape[1]), BF16)
    row = (mm(ones, high, NT) + mm(ones, low, NT))[:1]
    return row, jnp.sum(squares, axis=1, keepdims=True)


def kernel_of(cross, left, right):
    return jnp.exp((left + right - 2.0 * cross) * (-0.5 / FEATURES))


def selection(picked, start, size):
    return (iota((size, picked.shape[1]), 0) + start == picked).astype(BF16)


def coords():
    me = lax.axis_index("rows")
    core = lax.rem(me, 2)
    x = lax.rem(lax.div(me, STRIDE_X), NX)
    z = lax.rem(lax.div(me, STRIDE_Z), NZ)
    y = lax.div(me, STRIDE_Y)
    return me, core, x, y, z


def hops(size):
    return sorted(range(size), key=lambda d: -min(d, size - d))


def ring_peers(me, at, size, stride):
    out = []
    for hop in hops(size):
        if hop:
            position = lax.rem(at + hop, size)
            out.append((position, me + (position - at) * stride))
    return out


def plane_peers(me, x, y):
    pairs = [(dx, dy) for dx in range(NX) for dy in range(NY) if dx or dy]
    pairs.sort(key=lambda d: -(min(d[0], NX - d[0]) + min(d[1], NY - d[1])))
    out = []
    for dx, dy in pairs:
        px, py = lax.rem(x + dx, NX), lax.rem(y + dy, NY)
        out.append((py * NX + px, me + (px - x) * STRIDE_X + (py - y) * STRIDE_Y))
    return out


def aligned(start, size):
    return pl.ds(pl.multiple_of(start, size), size)


class Broadcast:
    def __init__(self, plane, z_ring, places, owner_places, refs, sems):
        self.plane, self.z_ring = plane, z_ring
        self.at, self.z = places
        self.owner_at, self.owner_z = owner_places
        self.whole, self.cand_p, self.cand_z, self.out = refs
        self.send, self.recv = sems

    def run(self, phase, source, target, peers, at):
        copies = []
        for position, device in peers:
            copies.append(
                pltpu.make_async_remote_copy(
                    source(position), target(at), self.send.at[phase, position],
                    self.recv.at[phase, at], device_id=(device,), device_id_type=MESH,
                )
            )
            copies[-1].start()

        def wait():
            for copy in copies:
                copy.wait_send()
            for position, device in peers:
                pltpu.make_async_remote_copy(
                    target(position), target(position), self.send.at[phase, position],
                    self.recv.at[phase, position], device_id=(device,), device_id_type=MESH,
                ).wait_recv()

        return wait

    def scatter(self):
        piece = self.cand_p.shape[1]
        wait = self.run(
            0, lambda p: self.whole.at[aligned(p * piece, piece), :], lambda p: self.cand_p.at[p],
            self.plane, self.at,
        )
        self.cand_p[self.at] = self.whole[aligned(self.at * piece, piece), :]
        return wait

    def exchange(self):
        self.cand_z[self.z] = self.cand_p[self.owner_at]
        return self.run(
            1, lambda p: self.cand_z.at[self.z], lambda p: self.cand_z.at[p], self.z_ring, self.z
        )

    def gather(self):
        piece = self.cand_p.shape[1]
        target = lambda p: self.out.at[aligned(p * piece, piece), :]
        self.out[aligned(self.at * piece, piece), :] = self.cand_z[self.owner_z]
        return self.run(2, lambda p: target(self.at), target, self.plane, self.at)


def inverse(matrix):
    n = matrix.shape[0]
    eye = (iota((n, n), 0) == iota((n, n), 1)).astype(F32)
    top = jnp.max(jnp.sum(jnp.abs(matrix), axis=0, keepdims=True), axis=1, keepdims=True)
    gain = 2.0 / (1.0 + top)
    rest = eye - gain * matrix
    scale = (top + 1.0) / jnp.maximum(top - 1.0, 1e-2)
    c = 1.0 + 1.0 / (2.0 * scale * scale - 1.0)
    result = (c * gain) * (eye + rest)
    parts = split(rest)
    for _ in range(STAGES - 1):
        rest = c * mm3(parts, parts) - (c - 1.0) * eye
        scale = jnp.minimum(2.0 * scale * scale - 1.0, 1e4)
        c = 1.0 + 1.0 / (2.0 * scale * scale - 1.0)
        parts = split(rest)
        result = c * (result + mm3(split(result), parts))
    return result


def block(k):
    return slice(k * NB, (k + 1) * NB)


def forward(k, v_ref, u_ref, xh_ref, xl_ref, wh_ref, wl_ref):
    v = split(v_ref[:, block(k)])
    if (k + 1) * NB < BLOCK:
        rest = slice((k + 1) * NB, BLOCK)
        v_ref[:, rest] = v_ref[:, rest] - mm3(v, (wh_ref[block(k), rest], wl_ref[block(k), rest]))
    u_ref[:, block(k)] = mm3(v, (xh_ref[k], xl_ref[k]))


def backward(u_ref, wh_ref, wl_ref):
    for j in range(BLOCK // NB - 1, 0, -1):
        u = split(u_ref[:, block(j)])
        for k in range(j):
            w = (wh_ref[block(k), block(j)], wl_ref[block(k), block(j)])
            u_ref[:, block(k)] = u_ref[:, block(k)] - mm3(u, w, NT)


def factor(points_ref, norm_row, norm_col, g_ref, xh_ref, xl_ref, wh_ref, wl_ref, after):
    count = BLOCK // NB
    for i in range(count):
        cross = mm(points_ref[block(i), :], points_ref[i * NB :, :], NT)
        tile = kernel_of(cross, norm_col[block(i)], norm_row[:, i * NB :])
        diagonal = (iota(tile.shape, 0) == iota(tile.shape, 1)).astype(F32)
        g_ref[block(i), i * NB :] = tile + RIDGE * diagonal
    for k in range(count):
        xh_ref[k], xl_ref[k] = split(inverse(g_ref[block(k), block(k)]))
        x = xh_ref[k], xl_ref[k]
        if k + 1 < count:
            rest = slice((k + 1) * NB, BLOCK)
            g = split(g_ref[block(k), rest])
            w = split(mm3(x, g))
            wh_ref[block(k), rest], wl_ref[block(k), rest] = w
            for i in range(k + 1, count):
                lo = (i - k - 1) * NB
                gi = (g[0][:, lo : lo + NB], g[1][:, lo : lo + NB])
                wi = (w[0][:, lo:], w[1][:, lo:])
                g_ref[block(i), i * NB :] = g_ref[block(i), i * NB :] - mm3(gi, wi, TN)
        after(k)


def updates_kernel(
    owner_ref, rows_ref, labels_ref, pred_ref, coef_ref, index_ref, points_ref, u_ref,
    own, got, whole_p, whole_r, cand_pp, cand_pz, cand_rp, cand_rz, res_ref,
    pts_ref, g_ref, xh_ref, xl_ref, wh_ref, wl_ref, v_ref, uf_ref, k12_ref, same_ref,
    send_p, recv_p, send_r, recv_r, send_c, recv_c,
):
    me, core, x, y, z = coords()
    other = me + 1 - 2 * core
    plane = plane_peers(me, x, y)
    z_ring = ring_peers(me, z, NZ, STRIDE_Z)

    barrier = pltpu.get_barrier_semaphore()
    pl.semaphore_signal(barrier, inc=1, device_id=(other,), device_id_type=MESH)
    for _, device in plane + z_ring:
        pl.semaphore_signal(barrier, inc=1, device_id=(device,), device_id_type=MESH)

    def across(number, source, target):
        return pltpu.make_async_remote_copy(
            source, target, send_c.at[number], recv_c.at[number],
            device_id=(other,), device_id_type=MESH,
        )

    high, low = split(residual_of(labels_ref[...], pred_ref[...], coef_ref[...]))
    left = jnp.concatenate([rows_ref[...].T, high, low], axis=0)

    def prepare(step):
        picked = index_ref[pl.ds(step, 1), :]
        acc = jnp.zeros((256, BLOCK), F32)
        for start in range(0, ROWS, 256):
            acc = acc + mm(left[:, start : start + 256], selection(picked, start, 256))
        acc = acc.astype(BF16)
        for b in range(8):
            own[0, b * 128 : (b + 1) * 128, :] = acc[:128, b * 128 : (b + 1) * 128]
            own[1, b * 128 : (b + 1) * 128, :] = acc[128:, b * 128 : (b + 1) * 128]

    owner = owner_ref[core]
    owner_core = lax.rem(owner, 2)
    owner_at = lax.div(owner, STRIDE_Y) * NX + lax.rem(lax.div(owner, STRIDE_X), NX)
    owner_z = lax.rem(lax.div(owner, STRIDE_Z), NZ)

    prepare(1 - core)
    pl.semaphore_wait(barrier, 1 + len(plane) + len(z_ring))
    send_points = across(0, own.at[0], got.at[0])
    send_points.start()
    send_residual = across(1, own.at[1], got.at[1])
    send_residual.start()
    send_points.wait()
    send_residual.wait()
    prepare(core)

    places, owner_places = (y * NX + x, z), (owner_at, owner_z)
    points = Broadcast(
        plane, z_ring, places, owner_places, (whole_p, cand_pp, cand_pz, pts_ref), (send_p, recv_p)
    )
    residual = Broadcast(
        plane, z_ring, places, owner_places, (whole_r, cand_rp, cand_rz, res_ref), (send_r, recv_r)
    )
    mine = owner_core == core
    whole_p[...] = jnp.where(mine, own[0], got[0])
    wait_p = points.scatter()
    whole_r[...] = jnp.where(mine, own[1], got[1])
    wait_p()
    wait_p = points.exchange()
    wait_r = residual.scatter()
    wait_p()
    wait_p = points.gather()
    wait_r()
    wait_r = residual.exchange()
    wait_p()
    for b in range(8):
        points_ref[core, b * 128 : (b + 1) * 128, :] = pts_ref[b * 128 : (b + 1) * 128, :].T
    share = across(2, points_ref.at[core], points_ref.at[core])
    share.start()
    wait_r()
    wait_r = residual.gather()

    my_points = points_ref.at[core]
    norm_row, norm_col = square_norms(my_points[...])

    def load_residual():
        part = lambda lo: jnp.concatenate(
            [res_ref[b * 128 + lo : b * 128 + lo + 64, :] for b in range(8)], axis=1
        )
        return part(0).astype(F32) + part(64).astype(F32)

    def after(k):
        if k == 0:
            wait_r()
            v_ref[...] = load_residual()
        forward(k, v_ref, uf_ref, xh_ref, xl_ref, wh_ref, wl_ref)

    factor(my_points, norm_row, norm_col, g_ref, xh_ref, xl_ref, wh_ref, wl_ref, after)
    share.wait()

    @pl.when(core == 0)
    def _():
        backward(uf_ref, wh_ref, wl_ref)
        u_ref[0, 0:TARGETS, :], u_ref[0, TARGETS:, :] = split(uf_ref[...])
        send = across(3, u_ref.at[0], u_ref.at[0])
        send.start()
        send.wait_send()
        across(4, u_ref.at[1], u_ref.at[1]).wait_recv()

    @pl.when(core == 1)
    def _():
        both = owner_ref[0] == owner_ref[1]
        _, left_col = square_norms(points_ref[0])
        first = index_ref[0:1, :].astype(F32)
        for i in range(0, BLOCK, 128):
            rows = slice(i, i + 128)
            cross = mm(points_ref[0, rows, :], points_ref[1], NT)
            column = jnp.broadcast_to(first[:, rows], (128, 128)).T[:, 0:1].astype(I32)
            same = ((column == index_ref[1:2, :]) & both).astype(BF16)
            same_ref[rows, :] = same
            k12_ref[rows, :] = kernel_of(cross, left_col[rows], norm_row).astype(BF16) + same
        v_ref[...] = load_residual()
        across(3, u_ref.at[0], u_ref.at[0]).wait_recv()
        v_ref[...] = v_ref[...] - (
            mm(u_ref[0, 0:TARGETS, :], k12_ref[...]) + mm(u_ref[0, TARGETS:, :], same_ref[...])
        )
        for k in range(BLOCK // NB):
            forward(k, v_ref, uf_ref, xh_ref, xl_ref, wh_ref, wl_ref)
        backward(uf_ref, wh_ref, wl_ref)
        u_ref[1, 0:TARGETS, :], u_ref[1, TARGETS:, :] = split(uf_ref[...])
        send = across(4, u_ref.at[1], u_ref.at[1])
        send.start()
        send.wait_send()


def place(update, picked):
    return jnp.concatenate(
        [mm(update, selection(picked, start, 256), NT) for start in range(0, ROWS, 256)], axis=1
    )


def apply_kernel(
    owner_ref, rows_ref, labels_ref, pred_ref, coef_ref, index_ref, block_ref, half_ref,
    new_pred_ref, new_coef_ref, sums_ref,
):
    me = lax.axis_index("rows")
    right, _ = square_norms(rows_ref[...])
    new_coef_ref[...] = coef_ref[...]
    columns = []
    for step in range(2):

        @pl.when(owner_ref[step] == me)
        def _():
            both = place(half_ref[step], index_ref[step : step + 1, :])
            new_coef_ref[...] = new_coef_ref[...] + (both[:TARGETS] + both[TARGETS:])

        _, left = square_norms(block_ref[step])
        before = pred_ref if step == 0 else new_pred_ref
        total = jnp.zeros((TARGETS, 1), F32)
        for start in range(0, ROWS, 256):
            cols = slice(start, start + 256)
            cross = mm(block_ref[step], rows_ref[cols, :], NT)
            half = kernel_of(cross, left, right[:, cols]).astype(BF16)
            new = before[:, cols] + mm(half_ref[step, 0:TARGETS, :], half)
            new_pred_ref[:, cols] = new
            residual = residual_of(labels_ref[:, cols], new, new_coef_ref[:, cols])
            total = total + jnp.sum(residual * residual, axis=1, keepdims=True)
        columns.append(total)
    sums = jnp.broadcast_to(jnp.concatenate(columns, axis=0), (128, 128))
    sums_ref[...] = sums.T[0:8, :]


def norm_kernel(total_rows, sums_ref, out_ref, got_a, got_y, got_z, send_sem, recv_sem):
    me, core, x, y, z = coords()
    here = core + 2 * x
    plane = []
    for hop in range(1, 2 * NX):
        position = lax.rem(here + hop, 2 * NX)
        plane.append((position, me + position - here))
    rings = (
        (plane, here, got_a),
        (ring_peers(me, y, NY, STRIDE_Y), y, got_y),
        (ring_peers(me, z, NZ, STRIDE_Z), z, got_z),
    )
    barrier = pltpu.get_barrier_semaphore()
    count = 0
    for ring, _, _ in rings:
        for _, device in ring:
            pl.semaphore_signal(barrier, inc=1, device_id=(device,), device_id_type=MESH)
            count += 1
    pl.semaphore_wait(barrier, count)
    value = sums_ref[...]
    for phase, (ring, at, got) in enumerate(rings):
        got[at] = value
        copies = []
        for position, device in ring:
            copy = pltpu.make_async_remote_copy(
                got.at[at], got.at[at], send_sem.at[phase, position], recv_sem.at[phase, at],
                device_id=(device,), device_id_type=MESH,
            )
            copy.start()
            copies.append(copy)
        for copy in copies:
            copy.wait_send()
        for position, device in ring:
            pltpu.make_async_remote_copy(
                got.at[position], got.at[position], send_sem.at[phase, position],
                recv_sem.at[phase, position], device_id=(device,), device_id_type=MESH,
            ).wait_recv()
        value = jnp.sum(got[...], axis=0)
    norms = jnp.sqrt(value / total_rows + 1e-06)
    out_ref[0:1, :] = norms[0:1, 0:TARGETS]
    out_ref[1:2, :] = norms[0:1, TARGETS:]


def local(embeddings, labels, predictions, coefficients, block_index, owner_id):
    shape = jax.ShapeDtypeStruct
    total_rows = embeddings.shape[0] * lax.axis_size("rows")
    labels = labels.reshape(1, ROWS)
    params = pltpu.CompilerParams(vmem_limit_bytes=VMEM_LIMIT)

    count = BLOCK // NB
    half = (BLOCK, 128)
    points, update = pl.pallas_call(
        updates_kernel,
        out_shape=[shape((2, BLOCK, FEATURES), BF16), shape((2, 2 * TARGETS, BLOCK), BF16)],
        in_specs=[smem()] + [vmem()] * 5,
        out_specs=[vmem()] * 2,
        scratch_shapes=[
            pltpu.VMEM((2,) + half, BF16),
            pltpu.VMEM((2,) + half, BF16),
            pltpu.VMEM(half, BF16),
            pltpu.VMEM(half, BF16),
            pltpu.VMEM((NX * NY, BLOCK // NX // NY, 128), BF16),
            pltpu.VMEM((NZ, BLOCK // NX // NY, 128), BF16),
            pltpu.VMEM((NX * NY, BLOCK // NX // NY, 128), BF16),
            pltpu.VMEM((NZ, BLOCK // NX // NY, 128), BF16),
            pltpu.VMEM(half, BF16),
            pltpu.VMEM(half, BF16),
            pltpu.VMEM((BLOCK, BLOCK), F32),
            pltpu.VMEM((count, NB, NB), BF16),
            pltpu.VMEM((count, NB, NB), BF16),
            pltpu.VMEM((BLOCK, BLOCK), BF16),
            pltpu.VMEM((BLOCK, BLOCK), BF16),
            pltpu.VMEM((TARGETS, BLOCK), F32),
            pltpu.VMEM((TARGETS, BLOCK), F32),
            pltpu.VMEM((BLOCK, BLOCK), BF16),
            pltpu.VMEM((BLOCK, BLOCK), BF16),
        ]
        + [pltpu.SemaphoreType.DMA((3, NX * NY))] * 4
        + [pltpu.SemaphoreType.DMA((5,))] * 2,
        compiler_params=pltpu.CompilerParams(
            collective_id=0, has_side_effects=True, vmem_limit_bytes=VMEM_LIMIT
        ),
        name="updates",
    )(owner_id, embeddings, labels, predictions, coefficients, block_index)

    new_pred, new_coef, sums = pl.pallas_call(
        apply_kernel,
        out_shape=[
            shape((TARGETS, ROWS), F32),
            shape((TARGETS, ROWS), F32),
            shape((8, 128), F32),
        ],
        in_specs=[smem()] + [vmem()] * 7,
        out_specs=[vmem()] * 3,
        compiler_params=params,
        name="apply",
    )(owner_id, embeddings, labels, predictions, coefficients, block_index, points, update)

    norms = pl.pallas_call(
        functools.partial(norm_kernel, total_rows),
        out_shape=shape((2, TARGETS), F32),
        in_specs=[vmem()],
        out_specs=vmem(),
        scratch_shapes=[
            pltpu.VMEM((2 * NX, 8, 128), F32),
            pltpu.VMEM((NY, 8, 128), F32),
            pltpu.VMEM((NZ, 8, 128), F32),
            pltpu.SemaphoreType.DMA((3, 8)),
            pltpu.SemaphoreType.DMA((3, 8)),
        ],
        compiler_params=pltpu.CompilerParams(collective_id=1, has_side_effects=True),
        name="norms",
    )(sums)
    return new_pred, new_coef, norms


def solution(mesh):
    in_specs = (P("rows", None), P("rows"), P(None, "rows"), P(None, "rows"), P(), P())
    out_specs = (P(None, "rows"), P(None, "rows"), P())
    return jax.shard_map(local, mesh=mesh, in_specs=in_specs, out_specs=out_specs, check_vma=False)
```

```python
import functools

import jax
import jax.numpy as jnp
from jax import lax
from jax.experimental import pallas as pl
from jax.experimental.pallas import tpu as pltpu
from jax.sharding import PartitionSpec as P

F32, BF16, I32 = jnp.float32, jnp.bfloat16, jnp.int32
MESH = pl.DeviceIdType.MESH
NN = (((1,), (0,)), ((), ()))
NT = (((1,), (1,)), ((), ()))
TN = (((0,), (0,)), ((), ()))

RIDGE = 1.0
LOG2E = 1.4426950408889634
FEATURES = 128
TARGETS = 64
BLOCK = 1024
ROWS = 2048
NX, NY, NZ = 4, 4, 8
STRIDE_X, STRIDE_Z, STRIDE_Y = 2, 2 * NX, 2 * NX * NZ
NB = 256
STAGES = 7
VMEM_LIMIT = 60 << 20


def mm(a, b, dims=NN):
    return lax.dot_general(a, b, dims, preferred_element_type=F32)


def split(a):
    high = a.astype(BF16)
    return high, (a - high.astype(F32)).astype(BF16)


def mm3(a, b, dims=NN):
    return mm(a[0], b[0], dims) + (mm(a[0], b[1], dims) + mm(a[1], b[0], dims))


def iota(shape, dim):
    return lax.broadcasted_iota(I32, shape, dim)


def vmem():
    return pl.BlockSpec(memory_space=pltpu.VMEM)


def smem():
    return pl.BlockSpec(memory_space=pltpu.SMEM)


def residual_of(labels, predictions, coefficients):
    targets = (labels <= iota((TARGETS, labels.shape[1]), 0)).astype(F32)
    return targets - predictions - RIDGE * coefficients


def augment(points):
    wide = points.astype(F32)
    high, low = split(wide * wide)
    ones = jnp.full((FEATURES, FEATURES), 0.5, BF16)
    half = mm(high, ones) + mm(low, ones)
    first, rest = half.astype(BF16), half
    rest = rest - first.astype(F32)
    second = rest.astype(BF16)
    third = (rest - second.astype(F32)).astype(BF16)
    lane = iota(half.shape, 1)
    parts = lambda at: jnp.where(
        lane == at, first.astype(F32),
        jnp.where(lane == at + 1, second.astype(F32),
                  jnp.where(lane == at + 2, third.astype(F32), 0.0)),
    )
    unit = lambda at: ((lane >= at) & (lane < at + 3)).astype(F32)
    left = (parts(0) + unit(3)).astype(BF16)
    right = (-unit(0) - parts(3)).astype(BF16)
    return jnp.concatenate([points, left], axis=1), jnp.concatenate([points, right], axis=1)


def kernel_of(left, right):
    return jnp.exp2(mm(left, right, NT) * (LOG2E / FEATURES))


def selection(picked, start, size):
    return (iota((size, picked.shape[1]), 0) + start == picked).astype(BF16)


def coords():
    me = lax.axis_index("rows")
    core = lax.rem(me, 2)
    x = lax.rem(lax.div(me, STRIDE_X), NX)
    z = lax.rem(lax.div(me, STRIDE_Z), NZ)
    y = lax.div(me, STRIDE_Y)
    return me, core, x, y, z


def hops(size):
    return sorted(range(size), key=lambda d: -min(d, size - d))


def ring_peers(me, at, size, stride):
    out = []
    for hop in hops(size):
        if hop:
            position = lax.rem(at + hop, size)
            out.append((position, me + (position - at) * stride))
    return out


def plane_peers(me, x, y):
    pairs = [(dx, dy) for dx in range(NX) for dy in range(NY) if dx or dy]
    pairs.sort(key=lambda d: -(min(d[0], NX - d[0]) + min(d[1], NY - d[1])))
    out = []
    for dx, dy in pairs:
        px, py = lax.rem(x + dx, NX), lax.rem(y + dy, NY)
        out.append((py * NX + px, me + (px - x) * STRIDE_X + (py - y) * STRIDE_Y))
    return out


def aligned(start, size):
    return pl.ds(pl.multiple_of(start, size), size)


class Broadcast:
    def __init__(self, plane, z_ring, places, owner_places, refs, sems):
        self.plane, self.z_ring = plane, z_ring
        self.at, self.z = places
        self.owner_at, self.owner_z = owner_places
        self.whole, self.cand_p, self.cand_z, self.out = refs
        self.send, self.recv = sems

    def run(self, phase, source, target, peers, at):
        copies = []
        for position, device in peers:
            copies.append(
                pltpu.make_async_remote_copy(
                    source(position), target(at), self.send.at[phase, position],
                    self.recv.at[phase, at], device_id=(device,), device_id_type=MESH,
                )
            )
            copies[-1].start()

        def wait():
            for copy in copies:
                copy.wait_send()
            for position, device in peers:
                pltpu.make_async_remote_copy(
                    target(position), target(position), self.send.at[phase, position],
                    self.recv.at[phase, position], device_id=(device,), device_id_type=MESH,
                ).wait_recv()

        return wait

    def scatter(self):
        piece = self.cand_p.shape[1]
        wait = self.run(
            0, lambda p: self.whole.at[aligned(p * piece, piece), :], lambda p: self.cand_p.at[p],
            self.plane, self.at,
        )
        self.cand_p[self.at] = self.whole[aligned(self.at * piece, piece), :]
        return wait

    def exchange(self):
        self.cand_z[self.z] = self.cand_p[self.owner_at]
        return self.run(
            1, lambda p: self.cand_z.at[self.z], lambda p: self.cand_z.at[p], self.z_ring, self.z
        )

    def gather(self):
        piece = self.cand_p.shape[1]
        target = lambda p: self.out.at[aligned(p * piece, piece), :]
        self.out[aligned(self.at * piece, piece), :] = self.cand_z[self.owner_z]
        return self.run(2, lambda p: target(self.at), target, self.plane, self.at)


def inverse(matrix):
    n = matrix.shape[0]
    eye = (iota((n, n), 0) == iota((n, n), 1)).astype(F32)
    top = jnp.max(jnp.sum(jnp.abs(matrix), axis=0, keepdims=True), axis=1, keepdims=True)
    gain = 2.0 / (1.0 + top)
    rest = eye - gain * matrix
    scale = (top + 1.0) / jnp.maximum(top - 1.0, 1e-2)
    c = 1.0 + 1.0 / (2.0 * scale * scale - 1.0)
    result = (c * gain) * (eye + rest)
    parts = split(rest)
    for _ in range(STAGES - 1):
        rest = c * mm3(parts, parts) - (c - 1.0) * eye
        scale = jnp.minimum(2.0 * scale * scale - 1.0, 1e4)
        c = 1.0 + 1.0 / (2.0 * scale * scale - 1.0)
        parts = split(rest)
        result = c * (result + mm3(split(result), parts))
    return result


def block(k):
    return slice(k * NB, (k + 1) * NB)


def forward(k, v_ref, u_ref, xh_ref, xl_ref, wh_ref, wl_ref):
    v = split(v_ref[:, block(k)])
    if (k + 1) * NB < BLOCK:
        rest = slice((k + 1) * NB, BLOCK)
        v_ref[:, rest] = v_ref[:, rest] - mm3(v, (wh_ref[block(k), rest], wl_ref[block(k), rest]))
    u_ref[:, block(k)] = mm3(v, (xh_ref[k], xl_ref[k]))


def backward(u_ref, wh_ref, wl_ref):
    for j in range(BLOCK // NB - 1, 0, -1):
        u = split(u_ref[:, block(j)])
        for k in range(j):
            w = (wh_ref[block(k), block(j)], wl_ref[block(k), block(j)])
            u_ref[:, block(k)] = u_ref[:, block(k)] - mm3(u, w, NT)


def factor(left_ref, right_ref, g_ref, xh_ref, xl_ref, wh_ref, wl_ref, after):
    count = BLOCK // NB
    for i in range(count):
        tile = kernel_of(left_ref[block(i), :], right_ref[i * NB :, :])
        diagonal = (iota(tile.shape, 0) == iota(tile.shape, 1)).astype(F32)
        g_ref[block(i), i * NB :] = tile + RIDGE * diagonal
    for k in range(count):
        xh_ref[k], xl_ref[k] = split(inverse(g_ref[block(k), block(k)]))
        x = xh_ref[k], xl_ref[k]
        if k + 1 < count:
            rest = slice((k + 1) * NB, BLOCK)
            g = split(g_ref[block(k), rest])
            w = split(mm3(x, g))
            wh_ref[block(k), rest], wl_ref[block(k), rest] = w
            for i in range(k + 1, count):
                lo = (i - k - 1) * NB
                gi = (g[0][:, lo : lo + NB], g[1][:, lo : lo + NB])
                wi = (w[0][:, lo:], w[1][:, lo:])
                g_ref[block(i), i * NB :] = g_ref[block(i), i * NB :] - mm3(gi, wi, TN)
        after(k)


def descend_kernel(
    owner_ref, rows_ref, labels_ref, pred_ref, coef_ref, index_ref,
    new_pred_ref, new_coef_ref, sums_ref,
    own, got, whole_p, whole_r, cand_pp, cand_pz, cand_rp, cand_rz, pts_ref, res_ref,
    sel_ref, right_ref, points_ref, left_ref, mine_ref, u_ref,
    g_ref, xh_ref, xl_ref, wh_ref, wl_ref, v_ref, uf_ref, k12_ref, same_ref,
    got_c, got_p, got_z,
    send_p, recv_p, send_r, recv_r, send_n, recv_n, send_c, recv_c,
):
    me, core, x, y, z = coords()
    other = me + 1 - 2 * core
    plane = plane_peers(me, x, y)
    z_ring = ring_peers(me, z, NZ, STRIDE_Z)
    place_at = y * NX + x

    barrier = pltpu.get_barrier_semaphore()
    pl.semaphore_signal(barrier, inc=1, device_id=(other,), device_id_type=MESH)
    for _, device in plane + z_ring:
        pl.semaphore_signal(barrier, inc=1, device_id=(device,), device_id_type=MESH)

    def across(number, source, target):
        return pltpu.make_async_remote_copy(
            source, target, send_c.at[number], recv_c.at[number],
            device_id=(other,), device_id_type=MESH,
        )

    high, low = split(residual_of(labels_ref[...], pred_ref[...], coef_ref[...]))
    left = jnp.concatenate([rows_ref[...].T, high, low], axis=0)

    def prepare(slot, step):
        picked = index_ref[pl.ds(step, 1), :]
        acc = jnp.zeros((256, BLOCK), F32)
        for start in range(0, ROWS, 256):
            rows = slice(start, start + 256)
            chosen = selection(picked, start, 256)
            sel_ref[step, rows, :] = chosen
            acc = acc + mm(left[:, rows], chosen)
        acc = acc.astype(BF16)
        for b in range(8):
            own[slot, 0, b * 128 : (b + 1) * 128, :] = acc[:128, b * 128 : (b + 1) * 128]
            own[slot, 1, b * 128 : (b + 1) * 128, :] = acc[128:, b * 128 : (b + 1) * 128]

    owner = owner_ref[core]
    owner_core = lax.rem(owner, 2)
    owner_at = lax.div(owner, STRIDE_Y) * NX + lax.rem(lax.div(owner, STRIDE_X), NX)
    owner_z = lax.rem(lax.div(owner, STRIDE_Z), NZ)

    prepare(1, 1 - core)
    pl.semaphore_wait(barrier, 1 + len(plane) + len(z_ring))
    send_points = across(0, own.at[1, 0], got.at[0])
    send_points.start()
    send_residual = across(1, own.at[1, 1], got.at[1])
    send_residual.start()
    prepare(0, core)

    places, owner_places = (place_at, z), (owner_at, owner_z)
    points = Broadcast(
        plane, z_ring, places, owner_places, (whole_p, cand_pp, cand_pz, pts_ref), (send_p, recv_p)
    )
    residual = Broadcast(
        plane, z_ring, places, owner_places, (whole_r, cand_rp, cand_rz, res_ref), (send_r, recv_r)
    )
    mine = owner_core == core
    send_points.wait()
    whole_p[...] = jnp.where(mine, own[0, 0], got[0])
    wait_p = points.scatter()
    send_residual.wait()
    whole_r[...] = jnp.where(mine, own[0, 1], got[1])
    right_ref[...] = augment(rows_ref[...])[1]
    wait_p()
    wait_p = points.exchange()
    wait_r = residual.scatter()
    new_coef_ref[...] = coef_ref[...]
    wait_p()
    wait_p = points.gather()
    wait_r()
    wait_r = residual.exchange()
    wait_p()
    for b in range(8):
        points_ref[core, b * 128 : (b + 1) * 128, :] = pts_ref[b * 128 : (b + 1) * 128, :].T
    share = across(2, points_ref.at[core], points_ref.at[core])
    share.start()
    wait_r()
    wait_r = residual.gather()

    left_ref[core], mine_ref[...] = augment(points_ref[core])

    def load_residual():
        part = lambda lo: jnp.concatenate(
            [res_ref[b * 128 + lo : b * 128 + lo + 64, :] for b in range(8)], axis=1
        )
        return part(0).astype(F32) + part(64).astype(F32)

    def after(k):
        if k == 0:
            wait_r()
            v_ref[...] = load_residual()
        forward(k, v_ref, uf_ref, xh_ref, xl_ref, wh_ref, wl_ref)

    factor(left_ref.at[core], mine_ref, g_ref, xh_ref, xl_ref, wh_ref, wl_ref, after)
    share.wait()

    @pl.when(core == 0)
    def _():
        backward(uf_ref, wh_ref, wl_ref)
        u_ref[0, 0:TARGETS, :], u_ref[0, TARGETS:, :] = split(uf_ref[...])
        across(3, u_ref.at[0], u_ref.at[0]).start()

    left_ref[1 - core] = augment(points_ref[1 - core])[0]

    @pl.when(core == 1)
    def _():
        both = owner_ref[0] == owner_ref[1]
        first = index_ref[0:1, :].astype(F32)
        for i in range(0, BLOCK, 128):
            rows = slice(i, i + 128)
            column = jnp.broadcast_to(first[:, rows], (128, 128)).T[:, 0:1].astype(I32)
            same = ((column == index_ref[1:2, :]) & both).astype(BF16)
            same_ref[rows, :] = same
            k12_ref[rows, :] = kernel_of(left_ref[0, rows, :], mine_ref[...]).astype(BF16) + same
        v_ref[...] = load_residual()
        across(3, u_ref.at[0], u_ref.at[0]).wait_recv()
        v_ref[...] = v_ref[...] - (
            mm(u_ref[0, 0:TARGETS, :], k12_ref[...]) + mm(u_ref[0, TARGETS:, :], same_ref[...])
        )
        for k in range(BLOCK // NB):
            forward(k, v_ref, uf_ref, xh_ref, xl_ref, wh_ref, wl_ref)
        backward(uf_ref, wh_ref, wl_ref)
        u_ref[1, 0:TARGETS, :], u_ref[1, TARGETS:, :] = split(uf_ref[...])
        across(4, u_ref.at[1], u_ref.at[1]).start()

    columns = []
    for step in range(2):
        if step == 1:

            @pl.when(core == 0)
            def _():
                across(3, u_ref.at[0], u_ref.at[0]).wait_send()
                across(4, u_ref.at[1], u_ref.at[1]).wait_recv()

            @pl.when(core == 1)
            def _():
                across(4, u_ref.at[1], u_ref.at[1]).wait_send()

        owned = (owner_ref[step] == me).astype(F32)
        before = pred_ref if step == 0 else new_pred_ref
        total = jnp.zeros((TARGETS, 1), F32)
        for start in range(0, ROWS, 256):
            cols = slice(start, start + 256)
            half = kernel_of(left_ref[step], right_ref[cols, :]).astype(BF16)
            new = before[:, cols] + mm(u_ref[step, 0:TARGETS, :], half)
            new_pred_ref[:, cols] = new
            placed = mm(u_ref[step], sel_ref[step, cols, :], NT)
            coef = new_coef_ref[:, cols] + owned * (placed[:TARGETS] + placed[TARGETS:])
            new_coef_ref[:, cols] = coef
            rest = residual_of(labels_ref[:, cols], new, coef)
            total = total + jnp.sum(rest * rest, axis=1, keepdims=True)
        columns.append(total)

    value = jnp.broadcast_to(jnp.concatenate(columns, axis=0), (128, 128)).T[0:8, :]
    groups = ((((1 - core, other),), core, got_c), (plane, place_at, got_p), (z_ring, z, got_z))
    for phase, (peers, at, slots) in enumerate(groups):
        slots[at] = value
        copies = []
        for position, device in peers:
            copy = pltpu.make_async_remote_copy(
                slots.at[at], slots.at[at], send_n.at[phase, position], recv_n.at[phase, at],
                device_id=(device,), device_id_type=MESH,
            )
            copy.start()
            copies.append(copy)
        for copy in copies:
            copy.wait_send()
        for position, device in peers:
            pltpu.make_async_remote_copy(
                slots.at[position], slots.at[position], send_n.at[phase, position],
                recv_n.at[phase, position], device_id=(device,), device_id_type=MESH,
            ).wait_recv()
        value = jnp.sum(slots[...], axis=0)
    sums_ref[...] = value


def finish_kernel(total_rows, pred_ref, coef_ref, sums_ref, out_pred_ref, out_coef_ref, out_ref):
    out_pred_ref[...] = pred_ref[...]
    out_coef_ref[...] = coef_ref[...]
    norms = jnp.sqrt(sums_ref[0:1, :] / total_rows + 1e-06)
    out_ref[0:1, :] = norms[:, 0:TARGETS]
    out_ref[1:2, :] = norms[:, TARGETS:]


def local(embeddings, labels, predictions, coefficients, block_index, owner_id):
    shape = jax.ShapeDtypeStruct
    total_rows = embeddings.shape[0] * lax.axis_size("rows")
    count = BLOCK // NB
    chips = NX * NY
    wide = shape((TARGETS, ROWS), F32)

    def room(*dims, kind=BF16):
        return pltpu.VMEM(dims, kind)

    new_pred, new_coef, sums = pl.pallas_call(
        descend_kernel,
        out_shape=[wide, wide, shape((8, 128), F32)],
        in_specs=[smem()] + [vmem()] * 5,
        out_specs=[vmem()] * 3,
        scratch_shapes=[
            room(2, 2, BLOCK, 128),
            room(2, BLOCK, 128),
            room(BLOCK, 128),
            room(BLOCK, 128),
            room(chips, BLOCK // chips, 128),
            room(NZ, BLOCK // chips, 128),
            room(chips, BLOCK // chips, 128),
            room(NZ, BLOCK // chips, 128),
            room(BLOCK, 128),
            room(BLOCK, 128),
            room(2, ROWS, BLOCK),
            room(ROWS, 2 * FEATURES),
            room(2, BLOCK, FEATURES),
            room(2, BLOCK, 2 * FEATURES),
            room(BLOCK, 2 * FEATURES),
            room(2, 2 * TARGETS, BLOCK),
            room(BLOCK, BLOCK, kind=F32),
            room(count, NB, NB),
            room(count, NB, NB),
            room(BLOCK, BLOCK),
            room(BLOCK, BLOCK),
            room(TARGETS, BLOCK, kind=F32),
            room(TARGETS, BLOCK, kind=F32),
            room(BLOCK, BLOCK),
            room(BLOCK, BLOCK),
            room(2, 8, 128, kind=F32),
            room(chips, 8, 128, kind=F32),
            room(NZ, 8, 128, kind=F32),
        ]
        + [pltpu.SemaphoreType.DMA((3, chips))] * 6
        + [pltpu.SemaphoreType.DMA((5,))] * 2,
        compiler_params=pltpu.CompilerParams(
            collective_id=0, has_side_effects=True, vmem_limit_bytes=VMEM_LIMIT
        ),
        name="descend",
    )(owner_id, embeddings, labels.reshape(1, ROWS), predictions, coefficients, block_index)

    return pl.pallas_call(
        functools.partial(finish_kernel, total_rows),
        out_shape=[wide, wide, shape((2, TARGETS), F32)],
        in_specs=[vmem()] * 3,
        out_specs=[vmem()] * 3,
        name="finish",
    )(new_pred, new_coef, sums)


def solution(mesh):
    in_specs = (P("rows", None), P("rows"), P(None, "rows"), P(None, "rows"), P(), P())
    out_specs = (P(None, "rows"), P(None, "rows"), P())
    return jax.shard_map(local, mesh=mesh, in_specs=in_specs, out_specs=out_specs, check_vma=False)
```
